128 devices in a mesh: ctx: 16 (over z_hi, x, core), tp: 8 (over z_lo, y).
Axes of the slice: x: 4, y: 4, z: 4 (z_hi: 2, z_lo: 2; z = z_hi * 2 + z_lo), core: 2. Of those that a mesh axis runs over, the one named last changes fastest.
Arguments:
- query_gate: bfloat16 [32, 1048576], P('tp', 'ctx'), may hold values from -6 to 6
- key_branch: bfloat16 [32, 1048576], P('tp', 'ctx'), may hold values from -6 to 6
- value_branch: bfloat16 [32, 1048576], P('tp', 'ctx'), may hold values from -6 to 6
- long_filter: float32 [32, 1048576], P('tp', 'ctx'), may hold values from -0.005859375 to 0.005859375
- skip_gain: float32 [32], P('tp'), may hold values from 0.5 to 1.5
- out_weight: bfloat16 [32, 32], replicated, may hold values from -1 to 1
Outputs:
- mixed: bfloat16 [32, 1048576], P('tp', 'ctx')
The draws below stay inside these ranges and needn't reach their ends.
All inputs are finite; a program needn't handle non-finite values.
Results may differ from the reference program's by a relative error of at most 0.02.
Values may be sent and summed in bfloat16 or wider, within the bound.
A program may use at most 256 MiB of HBM per device.

```python
import jax
import jax.numpy as jnp

SEQ = 1048576
CHANNELS = 32


def levels(stream_key, shape, split, low, largest):
    factor_of, own = 1.0, jax.random.fold_in(stream_key, 6)
    for dim, shards_of in split:
        steps = jnp.exp(jax.random.uniform(jax.random.fold_in(own, dim), (shards_of,), jnp.float32, low / len(split), largest / len(split)))
        factor_of = factor_of * jnp.repeat(steps, shape[dim] // shards_of).reshape([-1 if axis == dim else 1 for axis in range(len(shape))])
    return factor_of


def bell_draw(own_key, dims, spread, most, split=(), kind=jnp.bfloat16):
    factor_of = levels(own_key, dims, split, -0.22, 0.18) if split else 1.0
    entries = jax.random.normal(own_key, dims, jnp.float32) * spread * factor_of
    return jnp.minimum(jnp.maximum(entries, -most), most).astype(kind)


def setup_inputs(seed: int = 0) -> dict:
    key_of = jax.random.split(jax.random.key(seed), 7)
    return {
        "query_gate": bell_draw(key_of[0], (CHANNELS, SEQ), 1.0, 6.0, ((0, 8), (1, 16))),
        "key_branch": bell_draw(key_of[1], (CHANNELS, SEQ), 1.0, 6.0, ((0, 8), (1, 16))),
        "value_branch": bell_draw(key_of[2], (CHANNELS, SEQ), 1.0, 6.0, ((0, 8), (1, 16))),
        "long_filter": bell_draw(key_of[3], (CHANNELS, SEQ), SEQ ** -0.5, 0.005859375, ((0, 8), (1, 16)), jnp.float32),
        "skip_gain": jnp.clip(0.5 + 1.0 * jax.random.uniform(key_of[4], (CHANNELS,), jnp.float32) ** levels(key_of[4], (CHANNELS,), ((0, 8),), -0.2, 0.2), 0.5, 1.5),
        "out_weight": bell_draw(key_of[5], (CHANNELS, CHANNELS), CHANNELS ** -0.5, 1.0),
    }


def reference(query_gate, key_branch, value_branch, long_filter, skip_gain, out_weight):
    signal = key_branch.astype(jnp.float32) * value_branch.astype(jnp.float32)
    fft_length = 2 * SEQ
    signal_spec = jnp.fft.rfft(signal, n=fft_length, axis=1)
    filter_spec = jnp.fft.rfft(long_filter, n=fft_length, axis=1)
    conv = jnp.fft.irfft(signal_spec * filter_spec, n=fft_length, axis=1)[:, :SEQ]
    gated = (query_gate.astype(jnp.float32) * (conv + skip_gain[:, None] * signal)).astype(jnp.bfloat16)
    mixed = jnp.dot(out_weight.T, gated, preferred_element_type=jnp.float32)
    return mixed.astype(jnp.bfloat16)
```

```python
import functools
import math

import jax
import jax.numpy as jnp
import ml_dtypes
import numpy as np
from jax import lax
from jax.experimental import pallas as pl
from jax.experimental.pallas import tpu as pltpu
from jax.sharding import PartitionSpec as P

CTX = 16
TP = 8
CH = 4
FA = 512
FB = 128
M = FA * FB
ROWS = FA // CTX
SLAB = FA // TP
BF = jnp.bfloat16
F32 = jnp.float32


def phase(numer, denom):
    ang = -2.0 * math.pi * (numer % denom) / denom
    return np.cos(ang), np.sin(ang)


@functools.cache
def tables():
    f1 = 4 * np.arange(FA, dtype=np.int64) + 1
    a_re, a_im = phase(f1[:, None] * np.arange(FA)[None, :], 4 * FA)
    fwd_a = np.concatenate([a_re, a_im], 0).astype(ml_dtypes.bfloat16)
    inv_a = np.ascontiguousarray(fwd_a.T)
    t_re, t_im = phase(f1[:, None] * np.arange(FB)[None, :], 4 * M)
    turn = np.stack([t_re, t_im]).astype(np.float32)
    b_re, b_im = phase(np.arange(FB)[:, None] * np.arange(FB)[None, :], FB)
    fwd_b = np.block([[b_re, b_im], [-b_im, b_re]]).astype(ml_dtypes.bfloat16)
    inv_b = np.ascontiguousarray(fwd_b.T)
    return fwd_a, inv_a, turn, fwd_b, inv_b


def dot(left, right):
    return jnp.dot(left, right, preferred_element_type=F32)


def forward_kernel(k_ref, v_ref, h_ref, fa_ref, tw_ref, fb_ref, out_ref, sig):
    sig[...] = k_ref[...].astype(F32) * v_ref[...].astype(F32)
    for c in range(CH):
        s = sig[pl.ds(c, FA, stride=CH), :].astype(BF)
        h = h_ref[pl.ds(c, FA, stride=CH), :].astype(BF)
        step = dot(fa_ref[...], jnp.concatenate([s, h], 1))
        for i, row in ((0, c), (1, CH + c)):
            a_re = step[:FA, i * FB : (i + 1) * FB]
            a_im = step[FA:, i * FB : (i + 1) * FB]
            z_re = a_re * tw_ref[0] - a_im * tw_ref[1]
            z_im = a_re * tw_ref[1] + a_im * tw_ref[0]
            z = jnp.concatenate([z_re.astype(BF), z_im.astype(BF)], 1)
            spec = dot(z, fb_ref[...]).astype(BF)
            out_ref[:, row] = spec.reshape(CTX, ROWS, 2 * FB)


def block_kernel(in_ref, out_ref):
    tile = 8
    for c in range(CH):

        @pl.loop(0, ROWS // 16)
        def _(i):
            r = pl.ds(pl.multiple_of(i * 16, 16), 16)
            for half in range(2):
                sl = slice(half * tile, half * tile + tile)
                g_re, g_im = [], []
                p_re = p_im = None
                for n in range(CTX):
                    blk = in_ref[n, CH + c, r, :][sl].astype(F32)
                    h_re, h_im = blk[:, :FB], blk[:, FB:]
                    if n == 0:
                        g_re.append(h_re)
                        g_im.append(h_im)
                    else:
                        g_re.append(h_re - p_im)
                        g_im.append(h_im + p_re)
                    p_re, p_im = h_re, h_im
                y_re = [None] * CTX
                y_im = [None] * CTX
                for n in range(CTX):
                    blk = in_ref[n, c, r, :][sl].astype(F32)
                    s_re, s_im = blk[:, :FB], blk[:, FB:]
                    for j in range(CTX - n):
                        t_re = s_re * g_re[j] - s_im * g_im[j]
                        t_im = s_re * g_im[j] + s_im * g_re[j]
                        o = n + j
                        y_re[o] = t_re if y_re[o] is None else y_re[o] + t_re
                        y_im[o] = t_im if y_im[o] is None else y_im[o] + t_im
                for n in range(CTX):
                    out_ref[n, c, pl.ds(pl.multiple_of(i * 16 + half * tile, tile), tile), :] = (
                        jnp.concatenate([y_re[n], y_im[n]], 1).astype(BF)
                    )


def inverse_kernel(skip_ref, y_ref, q_ref, k_ref, v_ref, ia_ref, tw_ref, ib_ref, out_ref, sig, gate):
    sig[...] = k_ref[...].astype(F32) * v_ref[...].astype(F32)
    gate[...] = q_ref[...].astype(F32)
    for pair in range(CH // 2):
        cols = []
        for c in (2 * pair, 2 * pair + 1):
            y = y_ref[:, c].reshape(FA, 2 * FB)
            w = dot(y, ib_ref[...]) * (1.0 / M)
            w_re, w_im = w[:, :FB], w[:, FB:]
            v_re = w_re * tw_ref[0] + w_im * tw_ref[1]
            v_im = w_im * tw_ref[0] - w_re * tw_ref[1]
            cols.append(jnp.concatenate([v_re.astype(BF), v_im.astype(BF)], 0))
        conv = dot(ia_ref[...], jnp.concatenate(cols, 1))
        for i, c in ((0, 2 * pair), (1, 2 * pair + 1)):
            s = sig[pl.ds(c, FA, stride=CH), :]
            q = gate[pl.ds(c, FA, stride=CH), :]
            gated = q * (conv[:, i * FB : (i + 1) * FB] + skip_ref[c] * s)
            out_ref[:, c] = gated.astype(BF).reshape(TP, SLAB, FB)


def iota(shape, dim):
    return lax.broadcasted_iota(jnp.int32, shape, dim)


def mix_kernel(w_ref, g_ref, out_ref):
    chans = TP * CH
    size = chans * 16
    row, col = iota((size, chans), 0), iota((size, chans), 1)
    pick_out = (row // 64 * CH + row % CH == col).astype(F32).astype(BF)
    spread = (iota((chans, size), 1) // 16 == iota((chans, size), 0)).astype(F32).astype(BF)
    w_t = w_ref[...].astype(F32).T.astype(BF)
    wide = dot(dot(pick_out, w_t).astype(BF), spread)
    same = iota((size, size), 0) // CH % 16 == iota((size, size), 1) % 16
    table = jnp.where(same, wide, 0.0).astype(BF)
    for g in range(SLAB // 16):
        x = g_ref[:, g * 16 : (g + 1) * 16, :].reshape(size, FB)
        out_ref[:, g * 64 : (g + 1) * 64, :] = dot(table, x).astype(BF).reshape(TP, 64, FB)


def rows_of(x):
    return x.reshape(CH, FA, FB).transpose(1, 0, 2).reshape(FA * CH, FB)


def vmem(n):
    return [pl.BlockSpec(memory_space=pltpu.VMEM)] * n


def params():
    return pltpu.CompilerParams(vmem_limit_bytes=48 * 1024 * 1024)


def local(query_gate, key_branch, value_branch, long_filter, skip_gain, out_weight):
    fwd_a, inv_a, turn, fwd_b, inv_b = (jnp.asarray(t) for t in tables())
    q, k, v, h = (rows_of(x) for x in (query_gate, key_branch, value_branch, long_filter))
    spec = pl.pallas_call(
        forward_kernel,
        out_shape=jax.ShapeDtypeStruct((CTX, 2 * CH, ROWS, 2 * FB), BF),
        in_specs=vmem(6),
        out_specs=pl.BlockSpec(memory_space=pltpu.VMEM),
        scratch_shapes=[pltpu.VMEM((CH * FA, FB), F32)],
        compiler_params=params(),
        name="forward",
    )(k, v, h, fwd_a, turn, fwd_b)
    spec = lax.all_to_all(spec, "ctx", split_axis=0, concat_axis=0, tiled=True)
    prod = pl.pallas_call(
        block_kernel,
        out_shape=jax.ShapeDtypeStruct((CTX, CH, ROWS, 2 * FB), BF),
        in_specs=vmem(1),
        out_specs=pl.BlockSpec(memory_space=pltpu.VMEM),
        compiler_params=params(),
        name="blocks",
    )(spec)
    prod = lax.all_to_all(prod, "ctx", split_axis=0, concat_axis=0, tiled=True)
    gated = pl.pallas_call(
        inverse_kernel,
        out_shape=jax.ShapeDtypeStruct((TP, CH, SLAB, FB), BF),
        in_specs=[pl.BlockSpec(memory_space=pltpu.SMEM)] + vmem(7),
        out_specs=pl.BlockSpec(memory_space=pltpu.VMEM),
        scratch_shapes=[pltpu.VMEM((CH * FA, FB), F32)] * 2,
        compiler_params=params(),
        name="inverse",
    )(skip_gain, prod, q, k, v, inv_a, turn, inv_b)
    gated = lax.all_to_all(gated, "tp", split_axis=0, concat_axis=0, tiled=True)
    mixed = pl.pallas_call(
        mix_kernel,
        out_shape=jax.ShapeDtypeStruct((TP, SLAB * CH, FB), BF),
        in_specs=vmem(2),
        out_specs=pl.BlockSpec(memory_space=pltpu.VMEM),
        compiler_params=params(),
        name="mix",
    )(out_weight, gated.reshape(TP * CH, SLAB, FB))
    mixed = lax.all_to_all(mixed, "tp", split_axis=0, concat_axis=0, tiled=True)
    return mixed.reshape(FA, CH, FB).transpose(1, 0, 2).reshape(CH, M)


def solution(mesh):
    placed = (P("tp", "ctx"), P("tp", "ctx"), P("tp", "ctx"), P("tp", "ctx"), P("tp"), P())
    return jax.shard_map(
        local, mesh=mesh, in_specs=placed, out_specs=P("tp", "ctx"), check_vma=False
    )
```
